32 devices in a mesh: group: 1, expert: 16 (over z, y, x), dp: 2 (over core).
Axes of the slice: x: 2, y: 2, z: 4, core: 2. Of those that a mesh axis runs over, the one named last changes fastest.
Arguments:
- tokens: bfloat16 [2048, 4096], P(('group', 'expert', 'dp')), may hold values from -6 to 6
- queries: bfloat16 [2048, 4096], P(('group', 'expert', 'dp')), may hold values from -6 to 6
- keys_local: bfloat16 [2048, 256], P(('group', 'expert', 'dp')), may hold values from -6 to 6
- values_local: bfloat16 [2048, 256], P(('group', 'expert', 'dp')), may hold values from -6 to 6
- prompt_keys: bfloat16 [1024, 256], P('group'), may hold values from -6 to 6
- prompt_values: bfloat16 [1024, 256], P('group'), may hold values from -6 to 6
- norm_gain: float32 [4096], replicated, may hold values from 0.25 to 1.75
- expert_ids: int32 [2048, 8], P(('group', 'expert', 'dp')), may hold values from 0 to 15, all different within a row; in each aligned block of 64 rows (0 to 63, 64 to 127, ...) at most 42 rows name the same one
- route_weight: float32 [2048, 8], P(('group', 'expert', 'dp')), may hold values from 0.05 to 1
- stored_gate: bfloat16 [16, 4096, 768], P('expert', None, 'dp'), may hold values from -0.09375 to 0.09375
- stored_up: bfloat16 [16, 4096, 768], P('expert', None, 'dp'), may hold values from -0.09375 to 0.09375
- stored_down: bfloat16 [16, 768, 4096], P('expert', 'dp'), may hold values from -0.21875 to 0.21875
- holder: int32 [16], replicated, may hold values from 0 to 15, as said below
Outputs:
- layer_out: bfloat16 [2048, 4096], P(('group', 'expert', 'dp'))
The draws below stay inside these ranges and needn't reach their ends.
Inputs may be any that keep to these rules, and one draw needn't show every extreme that they name: `expert_ids`: each row names 8 different experts. In the 64 rows of one device no expert is named more than 42 times, and in every draw some expert is named exactly 42 times in some device's rows. holder[s] is s or the slot 8 away (s + 16 / 2 modulo 16), holder[holder[s]] = s, and holder[0] = 8.
All inputs are finite; a program needn't handle non-finite values.
Results may differ from the reference program's by a relative error of at most 0.0055.
Values may be sent and summed in bfloat16 or wider, within the bound.
A program may use at most 192 MiB of HBM per device.

```python
import math
import jax
import jax.numpy as jnp
import numpy as np
from jax import lax

D = 4096
FFW = 768
HEADS = 32
KVH = 2
HD = 128
TOPK = 8
PREFIX = 1024
TOK_DEV = 64
EXPERTS = 16
SPLITS = 2
CAP = 42
TOKENS = 2048


def drawn_keys(key):
    base = jax.random.fold_in(key, 11)
    key_width = KVH * HD
    drawn = jnp.clip(jax.random.normal(jax.random.fold_in(base, 3), (PREFIX, key_width), jnp.float32), -5.5, 5.5)
    return drawn


def draw_prompt_keys(key, part):
    drawn = drawn_keys(key)
    return drawn.astype(jnp.bfloat16)


def draw_queries(key, part):
    base = jax.random.fold_in(key, 23)
    values = jnp.clip(jax.random.normal(base, (TOKENS, HEADS * HD), jnp.float32), -5.5, 5.5)
    return values.astype(jnp.bfloat16)


def draw_holder(key, part):
    half_count = EXPERTS // 2
    flags = jax.random.randint(jax.random.fold_in(key, 3), (half_count,), 0, 2)
    flags = flags.at[0].set(1)
    lower_half = jnp.arange(half_count) + flags * half_count
    upper_half = jnp.arange(half_count) + half_count - flags * half_count
    return jnp.concatenate([lower_half, upper_half]).astype(jnp.int32)


def steps_of(stream_key, dims, shards, smallest, top_value):
    level, own = 1.0, jax.random.fold_in(stream_key, 6)
    for dim, parts in shards:
        steps = jnp.exp(jax.random.uniform(jax.random.fold_in(own, dim), (parts,), jnp.float32, smallest / len(shards), top_value / len(shards)))
        level = level * jnp.repeat(steps, dims[dim] // parts).reshape([-1 if axis == dim else 1 for axis in range(len(dims))])
    return level


def routed_block(key, own, number, rows, number_of, top, most, skew):
    order = jax.random.permutation(key, number_of)
    packed, usual = load_shares(number_of, rows * top, most, skew, True), load_shares(number_of, rows * top, most, skew, False)
    places = jnp.arange(number_of)

    def named(sizes, rotation):
        used = int((sizes > 0).sum())
        fixed = max(1, used // 4)
        passed = fixed + (places - fixed + rotation * (used - fixed)) % max(1, number_of - fixed)
        return jnp.zeros((number_of,), jnp.int32).at[order[jnp.where(places < fixed, places, passed)]].set(jnp.asarray(sizes, jnp.int32))

    sizes = jnp.where(number % 4 == 0, named(packed, number // 4), named(usual, number - number // 4 - 1))
    mixed = jax.random.permutation(jax.random.fold_in(own, 3), number_of)
    giver, receiver = mixed[0:number_of // 2 * 2:2], mixed[1:number_of // 2 * 2:2]
    room = jnp.minimum(sizes[giver] - 1, most - sizes[receiver]) // 2
    room = jnp.where((giver == order[0]) | (receiver == order[0]) | (sizes[receiver] == 0), 0, jnp.maximum(room, 0))
    passed = jax.random.randint(jax.random.fold_in(own, 4), (number_of // 2,), 0, 1 << 20) % (room + 1)
    sizes = sizes.at[giver].add(-passed).at[receiver].add(passed)
    labels = jnp.searchsorted(jnp.cumsum(sizes), jnp.arange(rows * top), side="right").astype(jnp.int32)
    table = labels.reshape(top, rows).T
    table = table[jax.random.permutation(jax.random.fold_in(own, 1), rows)]
    rotation = jax.random.randint(jax.random.fold_in(own, 2), (rows, 1), 0, top)
    return jnp.take_along_axis(table, (jnp.arange(top)[None, :] + rotation) % top, axis=1)


def load_shares(number_of, total, reach, slope, full):
    portions = [(1 << 20) // math.isqrt(grade ** slope) + 1 for grade in range(1, number_of + 1)]
    largest = reach if full else min(reach, max(-(-total // number_of), total * portions[0] // sum(portions)))
    least = 1 if total - largest >= number_of - 1 else 0
    counts, surplus = [largest] + [least] * (number_of - 1), total - largest - least * (number_of - 1)
    while surplus > 0:
        movable = [i for i in range(1, number_of) if counts[i] < largest] or [i for i in range(1, number_of) if counts[i] < reach]
        whole, left = sum([portions[i] for i in movable]), surplus
        for i in movable:
            extra = min(reach - counts[i], max(1, left * portions[i] // whole), surplus)
            counts[i] = counts[i] + extra
            surplus = surplus - extra
    return np.array(counts)


def normal_values(own_key, dims, width, limit, shards=(), kind=jnp.bfloat16):
    drawn = jax.random.normal(own_key, dims, jnp.float32) * width
    if len(shards) > 0:
        drawn = steps_of(own_key, dims, shards, -0.22, 0.18) * drawn
    return jnp.clip(drawn, min=-limit, max=limit).astype(kind)


def setup_inputs(seed: int = 0, part: int = 0) -> dict:
    keys = jax.random.split(jax.random.key(seed), 14)
    part_splits = jax.random.split(jax.random.fold_in(keys[13], part), 14)
    tokens = normal_values(part_splits[0], (TOKENS, D), 1.0, 6.0, ((0, 32),))
    queries = draw_queries(jax.random.fold_in(jax.random.fold_in(keys[13], part), 71), part)
    keys_local = normal_values(part_splits[2], (TOKENS, KVH * HD), 1.0, 6.0, ((0, 32),))
    values_local = normal_values(part_splits[3], (TOKENS, KVH * HD), 1.0, 6.0, ((0, 32),))
    prompt_keys = draw_prompt_keys(jax.random.fold_in(jax.random.fold_in(keys[13], part), 71), part)
    prompt_values = normal_values(part_splits[5], (PREFIX, KVH * HD), 1.0, 6.0)
    norm_gain = jnp.clip(1.0 + 0.15 * jax.random.normal(keys[6], (D,), jnp.float32), 0.25, 1.75)
    expert_ids_keys = jax.random.split(jax.random.fold_in(part_splits[7], 1), TOKENS // TOK_DEV)
    expert_ids_turns = jax.random.permutation(jax.random.fold_in(part_splits[7], 3), TOKENS // TOK_DEV)
    expert_ids = jax.vmap(lambda own, number: routed_block(jax.random.fold_in(part_splits[7], 2), own, number, TOK_DEV, EXPERTS, TOPK, CAP, 2))(expert_ids_keys, expert_ids_turns).reshape((TOKENS, TOPK))
    route_weight = jnp.clip(jnp.exp(math.log(1.0) - 2.9957323 * jax.random.uniform(part_splits[8], (TOKENS, TOPK), jnp.float32) ** steps_of(part_splits[8], (TOKENS, TOPK), ((0, 32),), -0.2, 0.2)), 0.05, 1.0)
    stored_gate = normal_values(keys[9], (EXPERTS, D, FFW), D ** -0.5, 0.09375, ((0, 16), (2, 2)))
    stored_up = normal_values(keys[10], (EXPERTS, D, FFW), D ** -0.5, 0.09375, ((0, 16), (2, 2)))
    stored_down = normal_values(keys[11], (EXPERTS, FFW, D), FFW ** -0.5, 0.21875, ((0, 16), (1, 2)))
    holder = draw_holder(jax.random.fold_in(keys[13], 71), part)
    return dict(tokens=tokens, queries=queries, keys_local=keys_local, values_local=values_local, prompt_keys=prompt_keys, prompt_values=prompt_values, norm_gain=norm_gain, expert_ids=expert_ids, route_weight=route_weight, stored_gate=stored_gate, stored_up=stored_up, stored_down=stored_down, holder=holder)


def attend_block(queries, keys_local, values_local, prompt_keys, prompt_values):
    count_rows = queries.shape[0]
    grouping = HEADS // KVH
    query_all = queries.astype(jnp.float32).reshape(count_rows, KVH, grouping, HD)
    key_all = jnp.concatenate([prompt_keys, keys_local], 0).astype(jnp.float32).reshape(-1, KVH, HD)
    value_all = jnp.concatenate([prompt_values, values_local], 0).astype(jnp.float32).reshape(-1, KVH, HD)
    scores = jnp.einsum('tkgd,skd->kgts', query_all, key_all) * HD ** (-0.5)
    column = jnp.arange(key_all.shape[0], dtype=jnp.int32)
    row_index = jnp.arange(count_rows, dtype=jnp.int32)
    allowed = (column[None, :] < PREFIX) | (column[None, :] - PREFIX <= row_index[:, None])
    scores = jnp.where(allowed[None, None], scores, -jnp.inf)
    highest = lax.optimization_barrier(jnp.max(scores, axis=-1, keepdims=True))
    expons = jnp.exp(scores - highest)
    weights = expons / lax.optimization_barrier(jnp.sum(expons, axis=-1, keepdims=True))
    weights = lax.optimization_barrier(weights.astype(jnp.bfloat16)).astype(jnp.float32)
    context = jnp.einsum('kgts,skd->tkgd', weights, value_all)
    return context.reshape(count_rows, HEADS * HD)

def reference(tokens, queries, keys_local, values_local, prompt_keys, prompt_values, norm_gain, expert_ids, route_weight, stored_gate, stored_up, stored_down, holder):
    block_count = TOKENS // TOK_DEV

    def one_block(items):
        return attend_block(items[0], items[1], items[2], prompt_keys, prompt_values)
    context = lax.map(one_block, (queries.reshape(block_count, TOK_DEV, -1), keys_local.reshape(block_count, TOK_DEV, -1), values_local.reshape(block_count, TOK_DEV, -1)))
    context = context.reshape(TOKENS, D)
    widened = tokens.astype(jnp.float32)
    normed = (widened * lax.rsqrt(lax.optimization_barrier(jnp.mean(widened * widened, axis=-1, keepdims=True)) + 1e-06) * norm_gain.astype(jnp.float32)).astype(jnp.bfloat16)
    shares = route_weight / lax.optimization_barrier(jnp.sum(route_weight, axis=-1, keepdims=True))
    grouped_ids = expert_ids.reshape(block_count, TOK_DEV * TOPK)
    onehot = (grouped_ids[:, :, None] == jnp.arange(EXPERTS, dtype=jnp.int32)[None, None, :]).astype(jnp.int32)
    slot_of = lax.optimization_barrier(jnp.sum((jnp.cumsum(onehot, axis=1) - onehot) * onehot, axis=2)).reshape(-1).astype(jnp.int32)
    flat_ids = expert_ids.reshape(-1).astype(jnp.int32)
    assigned = jnp.arange(TOKENS * TOPK, dtype=jnp.int32)
    anchor = (assigned // (TOK_DEV * TOPK)).astype(jnp.int32)
    token_of = (assigned // TOPK).astype(jnp.int32)
    column_at = anchor * CAP + slot_of
    row_table = jnp.full((EXPERTS, block_count * CAP), TOKENS, jnp.int32).at[flat_ids, column_at].set(token_of)
    share_table = jnp.zeros((EXPERTS, block_count * CAP), jnp.float32).at[flat_ids, column_at].set(shares.reshape(-1))
    padded = jnp.concatenate([normed, jnp.zeros((1, D), jnp.bfloat16)], 0)
    unit_count = FFW // SPLITS

    def serve(carry, inputs):
        expert_id, rows_at, scaling = inputs
        source = holder[expert_id]
        picked = padded[rows_at]
        gate_w = stored_gate[source]
        up_w = stored_up[source]
        down_w = stored_down[source]
        summed = jnp.zeros((picked.shape[0], D), jnp.float32)
        for section in range(SPLITS):
            lower = section * unit_count
            gate_val = jnp.dot(picked, gate_w[:, lower:lower + unit_count], preferred_element_type=jnp.float32)
            up_val = jnp.dot(picked, up_w[:, lower:lower + unit_count], preferred_element_type=jnp.float32)
            hidden = (jax.nn.silu(gate_val) * up_val).astype(jnp.bfloat16)
            partial_out = jnp.dot(hidden, down_w[lower:lower + unit_count], preferred_element_type=jnp.float32)
            summed = summed + lax.optimization_barrier(partial_out.astype(jnp.bfloat16)).astype(jnp.float32)
        result = lax.optimization_barrier(summed.astype(jnp.bfloat16)).astype(jnp.float32)
        carry = carry.at[rows_at].add(scaling[:, None] * result, mode='drop')
        return (carry, None)
    mixture, _ = lax.scan(serve, jnp.zeros((TOKENS, D), jnp.float32), (jnp.arange(EXPERTS, dtype=jnp.int32), row_table, share_table))
    return (widened + context + mixture).astype(jnp.bfloat16)
```

```python
import jax
import jax.numpy as jnp
from jax import lax
from jax.experimental import pallas as pl
from jax.experimental.pallas import tpu as pltpu
from jax.sharding import PartitionSpec as P

HEADS = 32
KVH = 2
HD = 128
TOPK = 8
EXP_DEV = 1
PREFIX = 1024


def attend_rows(queries, keys_local, values_local, prompt_keys, prompt_values):
    count_rows = queries.shape[0]
    grouping = HEADS // KVH
    query_all = queries.reshape(count_rows, KVH, grouping, HD)
    key_all = jnp.concatenate([prompt_keys, keys_local], 0).reshape(-1, KVH, HD)
    value_all = jnp.concatenate([prompt_values, values_local], 0).reshape(-1, KVH, HD)
    scores = jnp.einsum(
        "tkgd,skd->kgts", query_all, key_all, preferred_element_type=jnp.float32
    ) * HD ** (-0.5)
    column = jnp.arange(key_all.shape[0], dtype=jnp.int32)
    row_index = jnp.arange(count_rows, dtype=jnp.int32)
    allowed = (column[None, :] < PREFIX) | (column[None, :] - PREFIX <= row_index[:, None])
    scores = jnp.where(allowed[None, None], scores, -jnp.inf)
    highest = jnp.max(scores, axis=-1, keepdims=True)
    expons = jnp.exp(scores - highest)
    weights = (expons / jnp.sum(expons, axis=-1, keepdims=True)).astype(jnp.bfloat16)
    context = jnp.einsum("kgts,skd->tkgd", weights, value_all, preferred_element_type=jnp.float32)
    return context.reshape(count_rows, HEADS * HD)


def expert_rows(picked, gate_w, up_w, down_w):
    gate_val = jnp.dot(picked, gate_w, preferred_element_type=jnp.float32)
    up_val = jnp.dot(picked, up_w, preferred_element_type=jnp.float32)
    hidden = (jax.nn.silu(gate_val) * up_val).astype(jnp.bfloat16)
    return jnp.dot(hidden, down_w, preferred_element_type=jnp.float32).astype(jnp.bfloat16)


def ffn_body(x_ref, w_ref, gate_ref, up_ref, down_ref, out_ref):
    rows = x_ref[...]
    gate_val = jnp.dot(rows, gate_ref[0], preferred_element_type=jnp.float32)
    up_val = jnp.dot(rows, up_ref[0], preferred_element_type=jnp.float32)
    hidden = gate_val / (1.0 + jnp.exp(-gate_val)) * up_val * w_ref[...]
    out_ref[...] = jnp.dot(
        hidden.astype(jnp.bfloat16), down_ref[0], preferred_element_type=jnp.float32
    ).astype(jnp.bfloat16)


def dense_ffn(rows, scale, gate_w, up_w, down_w):
    count, width = rows.shape[0], gate_w.shape[1]
    tile = 256
    return pl.pallas_call(
        ffn_body,
        grid=(count // tile,),
        out_shape=jax.ShapeDtypeStruct((count, width), jnp.bfloat16),
        in_specs=[
            pl.BlockSpec((tile, width), lambda i: (i, 0)),
            pl.BlockSpec((tile, 1), lambda i: (i, 0)),
            pl.BlockSpec(gate_w.shape, lambda i: (0, 0, 0), pipeline_mode=pl.Buffered(1)),
            pl.BlockSpec(up_w.shape, lambda i: (0, 0, 0), pipeline_mode=pl.Buffered(1)),
            pl.BlockSpec(down_w.shape, lambda i: (0, 0, 0), pipeline_mode=pl.Buffered(1)),
        ],
        out_specs=pl.BlockSpec((tile, width), lambda i: (i, 0)),
        compiler_params=pltpu.CompilerParams(
            dimension_semantics=("arbitrary",), vmem_limit_bytes=48 * 1024 * 1024
        ),
    )(rows, scale, gate_w, up_w, down_w)


def dense_mixture(normed, shares, expert_ids, gate_w, up_w, down_w, holder):
    owners = lax.axis_size("expert")
    axes = ("expert", "dp")
    named = expert_ids[:, :, None] == jnp.arange(owners, dtype=jnp.int32)[None, None, :]
    table = jnp.sum(jnp.where(named, shares[:, :, None], 0.0), axis=1)
    high = table.astype(jnp.bfloat16)
    low = (table - high.astype(jnp.float32)).astype(jnp.bfloat16)
    spread = lax.all_gather(jnp.concatenate([high, low], axis=1), axes, axis=0, tiled=True)
    rows = lax.all_gather(normed, axes, axis=0, tiled=True)
    mine = holder[lax.axis_index("expert")]
    pick = jnp.arange(2 * owners, dtype=jnp.int32) % owners == mine
    scale = jnp.sum(jnp.where(pick[None], spread.astype(jnp.float32), 0.0), axis=1, keepdims=True)
    partial_out = dense_ffn(rows, scale, gate_w, up_w, down_w)
    return lax.psum_scatter(partial_out, axes, scatter_dimension=0, tiled=True).astype(jnp.float32)


def local(
    tokens,
    queries,
    keys_local,
    values_local,
    prompt_keys,
    prompt_values,
    norm_gain,
    expert_ids,
    route_weight,
    stored_gate,
    stored_up,
    stored_down,
    holder,
):
    owners = lax.axis_size("expert")
    tok_count = tokens.shape[0]
    model_width = tokens.shape[1]
    capacity = min(tok_count, max(2, tok_count * TOPK * 4 // (3 * owners * EXP_DEV)))
    gate_w = stored_gate[0]
    up_w = stored_up[0]
    down_w = stored_down[0]
    context = attend_rows(queries, keys_local, values_local, prompt_keys, prompt_values)
    widened = tokens.astype(jnp.float32)
    normed = (
        widened * lax.rsqrt(jnp.mean(widened * widened, axis=-1, keepdims=True) + 1e-06) * norm_gain
    ).astype(jnp.bfloat16)
    shares = route_weight / jnp.sum(route_weight, axis=-1, keepdims=True)
    devices = owners * lax.axis_size("dp")
    if devices * tok_count <= 2 * lax.axis_size("dp") * owners * capacity:
        mixture = dense_mixture(
            normed, shares, expert_ids, stored_gate, stored_up, stored_down, holder
        )
        return (widened + context + mixture).astype(jnp.bfloat16)
    flat_ids = expert_ids.reshape(-1)
    onehot = (flat_ids[:, None] == jnp.arange(owners, dtype=jnp.int32)[None, :]).astype(jnp.int32)
    earlier = jnp.cumsum(onehot, axis=0) - onehot
    slot_of = jnp.sum(earlier * onehot, axis=1)
    places = (holder[flat_ids] * capacity + slot_of).reshape(tok_count, TOPK)
    chooser = (
        (jnp.arange(owners * capacity, dtype=jnp.int32)[:, None, None] == places[None])
        .any(axis=2)
        .astype(jnp.bfloat16)
    )
    send_rows = (
        jnp.dot(chooser, normed, preferred_element_type=jnp.float32)
        .astype(jnp.bfloat16)
        .reshape(owners, capacity, model_width)
    )
    both_rows = lax.all_gather(
        lax.all_to_all(send_rows, "expert", split_axis=0, concat_axis=0, tiled=True)[None],
        "dp",
        axis=0,
        tiled=True,
    )
    partial_out = expert_rows(both_rows.reshape(-1, model_width), gate_w, up_w, down_w)
    partial_out = partial_out.astype(jnp.float32).reshape(both_rows.shape)
    own_sum = lax.psum_scatter(
        partial_out.astype(jnp.bfloat16), "dp", scatter_dimension=0, tiled=True
    ).astype(jnp.float32)[0]
    results = lax.all_to_all(
        own_sum.astype(jnp.bfloat16), "expert", split_axis=0, concat_axis=0, tiled=True
    )
    gathered = results.reshape(owners * capacity, model_width)[places]
    mixture = jnp.einsum("tk,tkd->td", shares, gathered.astype(jnp.float32))
    return (widened + context + mixture).astype(jnp.bfloat16)


def solution(mesh):
    return jax.shard_map(
        local,
        mesh=mesh,
        in_specs=(
            P(("group", "expert", "dp"), None),
            P(("group", "expert", "dp"), None),
            P(("group", "expert", "dp"), None),
            P(("group", "expert", "dp"), None),
            P("group", None),
            P("group", None),
            P(),
            P(("group", "expert", "dp"), None),
            P(("group", "expert", "dp"), None),
            P("expert", None, "dp"),
            P("expert", None, "dp"),
            P("expert", "dp", None),
            P(),
        ),
        out_specs=P(("group", "expert", "dp"), None),
        check_vma=False,
    )
```
